512 devices in a mesh: sub: 8 (over z_hi, y), rng: 64 (over z_lo, x, core).
Axes of the slice: x: 4, y: 4, z: 16 (z_hi: 2, z_lo: 8; z = z_hi * 8 + z_lo), core: 2. Of those that a mesh axis runs over, the one named last changes fastest.
Arguments:
- echoes: bfloat16 [2, 4096, 32768], P(None, ('sub', 'rng')), may hold values from -6 to 6
- fore_flag: int32 [3, 8, 64], P(None, None, 'rng'), may hold values from 0 to 1, as said below
- band_offset: int32 [3, 8, 64], P(None, None, 'rng'), may hold values from -16 to 16, as said below
- angle_interp: bfloat16 [3, 2, 512, 256], replicated, may hold values from -1 to 1
- range_kernel: bfloat16 [3, 544, 512], replicated, may hold values from -1 to 2, as said below
- center_shift: float32 [3, 8], replicated, may hold values from -6 to 6
Outputs:
- focused_image: float32 [2, 4096, 32768], P(None, 'sub', 'rng')
The draws below stay inside these ranges and needn't reach their ends.
Inputs may be any that keep to these rules, and one draw needn't show every extreme that they name: fore_flag[l, g, b] + fore_flag[l, g XOR 2**l, b] = 1 for every level l, group g and block b. `band_offset`: in every level both -16 and 16 occur. range_kernel[l, w, r] = 0 wherever |w - 16 - r| > 16.
All inputs are finite; a program needn't handle non-finite values.
Results may differ from the reference program's by a relative error of at most 0.0076.
Values may be sent and summed in bfloat16 or wider, within the bound.
A program may use at most 64 MiB of HBM per device.

```python
import math
import jax
import jax.numpy as jnp

ANGLES = 512
PULSES = 512
BLOCK_BINS = 512
BAND_HALF = 16
MAX_SHIFT = 16
RIM_WIDTH = 32
HALF_ANGLES = 256
LEVELS = 3
ALL_PULSES = 4096
ALL_BINS = 32768
N_SUB = 8
N_RNG = 64


def draw_fore_flag(key, part):
    sub_key = jax.random.fold_in(key, 5)
    coin_flips = jax.random.randint(sub_key, (LEVELS, N_SUB, N_RNG), 0, 2)
    group_ids = jnp.arange(N_SUB)
    level_rows = []
    for tree_level in range(LEVELS):
        stride = 2 ** tree_level
        upper_side = group_ids // stride % 2
        lower_group = group_ids - upper_side * stride
        level_rows.append((coin_flips[tree_level][lower_group] + upper_side[:, None]) % 2)
    return jnp.stack(level_rows).astype(jnp.int32)


def draw_band_offset(key, part):
    first_key, second_key, third_key = jax.random.split(jax.random.fold_in(key, 11), 3)
    cell_count = N_SUB * N_RNG
    shifts = jax.random.randint(first_key, (LEVELS, cell_count), -MAX_SHIFT, MAX_SHIFT + 1)
    top_pos = jax.random.randint(second_key, (LEVELS, 1), 0, cell_count)
    spacing = jax.random.randint(third_key, (LEVELS, 1), 1, cell_count)
    bottom_pos = (top_pos + spacing) % cell_count
    positions = jnp.arange(cell_count)[None, :]
    shifts = jnp.where(positions == top_pos, MAX_SHIFT, shifts)
    shifts = jnp.where(positions == bottom_pos, -MAX_SHIFT, shifts)
    return shifts.reshape(LEVELS, N_SUB, N_RNG).astype(jnp.int32)


def draw_angle_interp(key, part):
    sub_key = jax.random.fold_in(key, 23)
    parent = jnp.arange(ANGLES)[:, None]
    child_ids = jnp.arange(HALF_ANGLES)[None, :]
    nearest = jnp.where(child_ids == parent // 2, 0.55, 0.0).astype(jnp.float32)
    shape = (LEVELS, 2, ANGLES, HALF_ANGLES)
    jitter = 0.35 * jnp.clip(jax.random.normal(sub_key, shape, jnp.float32), -4.0, 4.0)
    return (nearest + jitter / math.sqrt(HALF_ANGLES)).astype(jnp.bfloat16)


def draw_range_kernel(key, part):
    sub_key = jax.random.fold_in(key, 37)
    row_ids = jnp.arange(BLOCK_BINS + 2 * BAND_HALF)[:, None]
    col_ids = jnp.arange(BLOCK_BINS)[None, :]
    offset = row_ids - BAND_HALF - col_ids
    inband = (jnp.abs(offset) <= BAND_HALF).astype(jnp.float32)
    diagonal = (offset == 0).astype(jnp.float32)
    shape = (LEVELS, BLOCK_BINS + 2 * BAND_HALF, BLOCK_BINS)
    jitter = 0.35 * jnp.clip(jax.random.normal(sub_key, shape, jnp.float32), -4.0, 4.0)
    return (diagonal + inband * jitter / math.sqrt(2 * BAND_HALF + 1)).astype(jnp.bfloat16)


def shard_levels(stream_key, shape, cuts, low, top_value):
    def one(position, parts):
        heights = jax.random.uniform(jax.random.fold_in(jax.random.fold_in(stream_key, 6), position), (parts,), jnp.float32, low / len(cuts), top_value / len(cuts))
        return jnp.repeat(jnp.exp(heights), shape[position] // parts).reshape((-1,) + (1,) * (len(shape) - position - 1))

    factor_of = one(*cuts[0])
    for cut in cuts[1:]:
        factor_of = factor_of * one(*cut)
    return factor_of


def bell_draw(own_key, shape, width, reach, cuts=(), kind=jnp.bfloat16):
    result = jax.random.normal(own_key, shape, jnp.float32) * width
    if len(cuts) > 0:
        result = shard_levels(own_key, shape, cuts, -0.22, 0.18) * result
    return jnp.clip(result, min=-reach, max=reach).astype(kind)


def setup_inputs(seed: int = 0) -> dict:
    seeds = jax.random.split(jax.random.key(seed), 7)
    return {
        "echoes": bell_draw(seeds[0], (2, ALL_PULSES, ALL_BINS), 1.0, 6.0, ((1, 512),)),
        "fore_flag": draw_fore_flag(jax.random.fold_in(seeds[6], 71), 0),
        "band_offset": draw_band_offset(jax.random.fold_in(seeds[6], 71), 0),
        "angle_interp": draw_angle_interp(jax.random.fold_in(seeds[6], 71), 0),
        "range_kernel": draw_range_kernel(jax.random.fold_in(seeds[6], 71), 0),
        "center_shift": jnp.clip(jax.random.uniform(seeds[5], (LEVELS, N_SUB), jnp.float32, -6.0, 6.0), -6.0, 6.0),
    }


def doppler_matrix(angles, pulses):
    angle_ids = jnp.arange(angles, dtype=jnp.int32)[:, None]
    pulse_ids = jnp.arange(pulses, dtype=jnp.int32)[None, :]
    cycles = (2 * angle_ids + 1 - angles) * pulse_ids % (2 * angles)
    phase_angle = math.pi / angles * cycles.astype(jnp.float32)
    cosine = jnp.cos(phase_angle) / math.sqrt(pulses)
    sine_part = jnp.sin(phase_angle) / math.sqrt(pulses)
    upper_rows = jnp.concatenate([cosine, sine_part], axis=1)
    bottom = jnp.concatenate([-sine_part, cosine], axis=1)
    return jnp.concatenate([upper_rows, bottom], axis=0).astype(jnp.bfloat16)

def phase_turn(real_imag, shift_rate, block_start, total_bins):
    angles = real_imag.shape[1]
    bin_count = real_imag.shape[2]
    angle_pos = (jnp.arange(angles).astype(jnp.float32)[:, None] + 0.5) / angles - 0.5
    range_pos = 1.0 + (block_start + jnp.arange(bin_count)).astype(jnp.float32)[None, :] / total_bins
    phase_angle = math.pi * shift_rate * angle_pos * range_pos
    cosine = jnp.cos(phase_angle)
    sine_part = jnp.sin(phase_angle)
    real_part = real_imag[0] * cosine - real_imag[1] * sine_part
    imag_part = real_imag[0] * sine_part + real_imag[1] * cosine
    return jnp.stack([real_part, imag_part])

def block_term(image, upper_sel, matrix_zero, matrix_one, use_one):
    blocks = image.reshape(2, ANGLES, N_RNG, BLOCK_BINS)
    rows = jnp.where(upper_sel, blocks[:, HALF_ANGLES:], blocks[:, :HALF_ANGLES]).astype(jnp.float32)
    term_zero = jnp.einsum('pa,cabr->cpbr', matrix_zero, rows)
    term_one = jnp.einsum('pa,cabr->cpbr', matrix_one, rows)
    return jnp.where(use_one, term_one, term_zero).reshape(2, ANGLES, ALL_BINS)

def reference(echoes, fore_flag, band_offset, angle_interp, range_kernel, center_shift):
    filter_matrix = doppler_matrix(ANGLES, PULSES)
    images = []
    for group_id in range(N_SUB):
        pulse_block = echoes[:, group_id * PULSES:(group_id + 1) * PULSES, :].reshape(2 * PULSES, ALL_BINS)
        filtered = jnp.dot(filter_matrix, pulse_block, preferred_element_type=jnp.float32)
        images.append(filtered.astype(jnp.bfloat16).reshape(2, ANGLES, ALL_BINS))
    window_ids = jnp.arange(BLOCK_BINS + 2 * BAND_HALF, dtype=jnp.int32)
    block_starts = jnp.arange(N_RNG, dtype=jnp.int32) * BLOCK_BINS + RIM_WIDTH - BAND_HALF
    for tree_level in range(LEVELS):
        kernel = range_kernel[tree_level].astype(jnp.float32)
        resampled = []
        for group_id in range(N_SUB):
            padded = jnp.pad(images[group_id], ((0, 0), (0, 0), (RIM_WIDTH, RIM_WIDTH)))
            starts = (block_starts + band_offset[tree_level, group_id]).astype(jnp.int32)
            window_index = (starts[:, None] + window_ids[None, :]).astype(jnp.int32)
            windows = padded[:, :, window_index].astype(jnp.float32)
            values = jnp.einsum('cabw,wr->cabr', windows, kernel)
            resampled.append(values.reshape(2, ANGLES, ALL_BINS).astype(jnp.bfloat16))
        matrix_zero = angle_interp[tree_level, 0].astype(jnp.float32)
        matrix_one = angle_interp[tree_level, 1].astype(jnp.float32)
        merged_list = []
        for group_id in range(N_SUB):
            partner = group_id ^ 1 << tree_level
            own_flag = fore_flag[tree_level, group_id]
            partner_flag = fore_flag[tree_level, partner]
            upper_sel = (own_flag == 1)[None, None, :, None]
            own_one = (own_flag == 1)[None, None, :, None]
            partner_one = (partner_flag == 1)[None, None, :, None]
            own_term = block_term(resampled[group_id], upper_sel, matrix_zero, matrix_one, own_one)
            partner_term = block_term(resampled[partner], upper_sel, matrix_zero, matrix_one, partner_one)
            merged = phase_turn(own_term, center_shift[tree_level, group_id], 0, ALL_BINS)
            merged = merged + phase_turn(partner_term, center_shift[tree_level, partner], 0, ALL_BINS)
            if tree_level + 1 < LEVELS:
                merged = merged.astype(jnp.bfloat16)
            merged_list.append(merged)
        images = merged_list
    return jnp.concatenate(images, axis=1)
```

```python
import functools
import math

import jax
import jax.numpy as jnp
import ml_dtypes
import numpy as np
from jax import lax
from jax.experimental import pallas as pl
from jax.experimental.pallas import tpu as pltpu
from jax.sharding import PartitionSpec as P

ANGLES = 512
PULSES = 512
BINS = 512
TILE = 128
TILES = BINS // TILE
HALF = ANGLES // 2
BAND_HALF = 16
LEVELS = 3
MESH = pl.DeviceIdType.MESH
ORDER = (1, 2, 0, 3)


def doppler_constant(sources):
    angle = np.arange(ANGLES, dtype=np.int64)[:, None]
    pulse = np.arange(PULSES, dtype=np.int64)[None, :]
    cycles = (2 * angle + 1 - ANGLES) * pulse % (2 * ANGLES)
    phase = math.pi / ANGLES * cycles
    cosine = np.cos(phase) / math.sqrt(PULSES)
    sine = np.sin(phase) / math.sqrt(PULSES)
    whole = np.block([[cosine, sine], [-sine, cosine]])
    whole = whole.reshape(2 * ANGLES, 2, sources, PULSES // sources)
    return whole.transpose(0, 2, 1, 3).reshape(2 * ANGLES, 2 * PULSES).astype(ml_dtypes.bfloat16)


def kernel(
    sources,
    total_bins,
    echoes,
    doppler,
    kernels,
    interp,
    flags,
    offsets,
    shifts,
    out,
    turned,
    wide,
    shifted,
    chosen,
    images,
    left_rim,
    right_rim,
    given,
    kept,
    taken,
    total,
    cos_table,
    sin_table,
    turn_sem,
    wide_sem,
    rim_send,
    rim_recv,
    pair_send,
    pair_recv,
    out_sem,
):
    group = lax.axis_index("sub")
    block = lax.axis_index("rng")
    partners = [jnp.bitwise_xor(group, 1 << level) for level in range(LEVELS)]

    barrier = pltpu.get_barrier_semaphore()

    def greet(step, carry):
        peer = lax.rem(block + step, sources)
        pl.semaphore_signal(barrier, inc=1, device_id=(group, peer), device_id_type=MESH)
        return carry

    for partner in partners[::-1]:
        pl.semaphore_signal(barrier, inc=1, device_id=(partner, block), device_id_type=MESH)
    lax.fori_loop(1, sources, greet, 0)
    load = pltpu.make_async_copy(doppler, wide, wide_sem)
    load.start()
    pl.semaphore_wait(barrier, sources - 1 + LEVELS)

    def turn(step, carry):
        peer = lax.rem(block + step, sources)
        pltpu.make_async_remote_copy(
            src_ref=echoes.at[:, pl.ds(pl.multiple_of(peer * BINS, BINS), BINS)],
            dst_ref=turned.at[block],
            send_sem=turn_sem.at[0],
            recv_sem=turn_sem.at[1],
            device_id=(group, peer),
            device_id_type=MESH,
        ).start()
        return carry

    lax.fori_loop(1, sources, turn, 0)
    stay = pltpu.make_async_copy(
        echoes.at[:, pl.ds(pl.multiple_of(block * BINS, BINS), BINS)], turned.at[block], turn_sem.at[2]
    )
    stay.start()

    for level in range(LEVELS):
        offset = offsets[level, group]
        rows = lax.broadcasted_iota(jnp.int32, (TILE, BINS + 2 * BAND_HALF), 0)
        taps = lax.broadcasted_iota(jnp.int32, (TILE, BINS + 2 * BAND_HALF), 1)

        def shift(step, carry, level=level, offset=offset, rows=rows, taps=taps):
            start = pl.multiple_of(step * TILE, TILE)
            pick = jnp.where(rows + start == taps + (TILE - BAND_HALF + offset), 1.0, 0.0).astype(jnp.bfloat16)
            moved = jnp.dot(pick, kernels[level], preferred_element_type=jnp.float32)
            shifted[level, pl.ds(start, TILE), :] = moved.astype(jnp.bfloat16)
            return carry

        lax.fori_loop(0, TILES + 2, shift, 0)

        def choose(step, carry, level=level):
            rows = pl.ds(pl.multiple_of(step * TILE, TILE), TILE)
            zero = interp[level, 0, rows, :].astype(jnp.float32)
            one = interp[level, 1, rows, :].astype(jnp.float32)
            side = jnp.full((TILE, HALF), flags[level, group], jnp.int32)
            chosen[level, 0, rows, :] = jnp.where(side == 1, one, zero).astype(jnp.bfloat16)
            chosen[level, 1, rows, :] = jnp.where(side == 1, zero, one).astype(jnp.bfloat16)
            return carry

        lax.fori_loop(0, ANGLES // TILE, choose, 0)

    rows_at_once = 32

    def tables(step, carry):
        first = pl.multiple_of(step * rows_at_once, rows_at_once)
        angle = lax.broadcasted_iota(jnp.int32, (rows_at_once, BINS), 0) + first
        angle_pos = (angle.astype(jnp.float32) + 0.5) / ANGLES - 0.5
        bins = lax.broadcasted_iota(jnp.int32, (rows_at_once, BINS), 1) + block * BINS
        range_pos = 1.0 + bins.astype(jnp.float32) / total_bins
        for level in range(LEVELS):
            for side, owner in enumerate((group, partners[level])):
                phase = math.pi * shifts[level, owner] * angle_pos * range_pos
                cos_table[level, side, pl.ds(first, rows_at_once), :] = jnp.cos(phase)
                sin_table[level, side, pl.ds(first, rows_at_once), :] = jnp.sin(phase)
        return carry

    lax.fori_loop(0, ANGLES // rows_at_once, tables, 0)

    @pl.when(block == 0)
    def _():
        for level in range(LEVELS):
            left_rim[level] = jnp.zeros((2 * ANGLES, TILE), jnp.bfloat16)

    @pl.when(block == sources - 1)
    def _():
        for level in range(LEVELS):
            right_rim[level] = jnp.zeros((2 * ANGLES, TILE), jnp.bfloat16)

    def to_left(level):
        return pltpu.make_async_remote_copy(
            src_ref=images.at[level, :, pl.ds(0, TILE)],
            dst_ref=right_rim.at[level],
            send_sem=rim_send.at[level, 0],
            recv_sem=rim_recv.at[level, 0],
            device_id=(group, block - 1),
            device_id_type=MESH,
        )

    def to_right(level):
        return pltpu.make_async_remote_copy(
            src_ref=images.at[level, :, pl.ds(BINS - TILE, TILE)],
            dst_ref=left_rim.at[level],
            send_sem=rim_send.at[level, 1],
            recv_sem=rim_recv.at[level, 1],
            device_id=(group, block + 1),
            device_id_type=MESH,
        )

    def send_rims(level, left=True, right=True):
        if left:

            @pl.when(block > 0)
            def _():
                to_left(level).start()

        if right:

            @pl.when(block < sources - 1)
            def _():
                to_right(level).start()

    load.wait()
    stay.wait()
    others = turned.at[pl.ds(0, sources - 1)]
    pltpu.make_async_copy(others, others, turn_sem.at[1]).wait()
    pltpu.make_async_copy(others, others, turn_sem.at[0]).wait()

    def filtering(step, carry):
        start = pl.multiple_of(step * TILE, TILE)
        stack = turned[...].reshape(2 * PULSES, BINS)
        image = jnp.dot(wide[pl.ds(start, TILE), :], stack, preferred_element_type=jnp.float32)
        images[0, pl.ds(start, TILE), :] = image.astype(jnp.bfloat16)
        return carry

    lax.fori_loop(0, 2 * ANGLES // TILE, filtering, 0)
    send_rims(0)

    for level in range(LEVELS):
        flag = flags[level, group]

        def split(values):
            side = jnp.full(values[0].shape, flag, jnp.int32)
            give = jnp.where(side == 1, values[0], values[1]).astype(jnp.bfloat16)
            keep = jnp.where(side == 1, values[1], values[0]).astype(jnp.bfloat16)
            return give, keep

        def rows_of(part):
            return [slice(part * ANGLES + side * HALF, part * ANGLES + side * HALF + HALF) for side in range(2)]

        def middle(part, level=level):
            return [
                jnp.dot(
                    images[level, rows, :],
                    shifted[level, TILE : TILE + BINS, TILE : 3 * TILE],
                    preferred_element_type=jnp.float32,
                )
                for rows in rows_of(part)
            ]

        def first(part, level=level):
            return [
                jnp.dot(
                    images[level, rows, 0 : 2 * TILE],
                    shifted[level, TILE : 3 * TILE, 0:TILE],
                    preferred_element_type=jnp.float32,
                )
                + jnp.dot(left_rim[level, rows, :], shifted[level, 0:TILE, 0:TILE], preferred_element_type=jnp.float32)
                for rows in rows_of(part)
            ]

        def last(part, level=level):
            return [
                jnp.dot(
                    images[level, rows, BINS - 2 * TILE : BINS],
                    shifted[level, BINS - TILE : BINS + TILE, BINS - TILE : BINS],
                    preferred_element_type=jnp.float32,
                )
                + jnp.dot(
                    right_rim[level, rows, :],
                    shifted[level, BINS + TILE : BINS + 2 * TILE, BINS - TILE : BINS],
                    preferred_element_type=jnp.float32,
                )
                for rows in rows_of(part)
            ]

        def to_partner(tile, level=level):
            return pltpu.make_async_remote_copy(
                src_ref=given.at[level, tile],
                dst_ref=taken.at[level, tile],
                send_sem=pair_send.at[level, tile],
                recv_sem=pair_recv.at[level, tile],
                device_id=(partners[level], block),
                device_id_type=MESH,
            )

        for part in range(2):
            give, keep = split(middle(part))
            given[level, 1, part] = give[:, 0:TILE]
            given[level, 2, part] = give[:, TILE : 2 * TILE]
            kept[part, :, TILE : 3 * TILE] = keep
        to_partner(1).start()
        to_partner(2).start()

        @pl.when(block > 0)
        def _(level=level):
            to_right(level).wait_recv()

        for part in range(2):
            given[level, 0, part], kept[part, :, 0:TILE] = split(first(part))
        to_partner(0).start()

        @pl.when(block < sources - 1)
        def _(level=level):
            to_left(level).wait_recv()

        for part in range(2):
            given[level, 3, part], kept[part, :, BINS - TILE : BINS] = split(last(part))
        to_partner(3).start()

        def own(step, carry, level=level):
            rows = pl.ds(pl.multiple_of(step * TILE, TILE), TILE)
            low_rows = pl.ds(pl.multiple_of(step * TILE + ANGLES, TILE), TILE)
            matrix = chosen[level, 0, rows, :]
            real = jnp.dot(matrix, kept[0], preferred_element_type=jnp.float32)
            imag = jnp.dot(matrix, kept[1], preferred_element_type=jnp.float32)
            cosine = cos_table[level, 0, rows, :]
            sine = sin_table[level, 0, rows, :]
            total[rows, :] = real * cosine - imag * sine
            total[low_rows, :] = real * sine + imag * cosine
            return carry

        lax.fori_loop(0, ANGLES // TILE, own, 0)

        for tile in ORDER:
            columns = slice(tile * TILE, tile * TILE + TILE)
            to_partner(tile).wait_recv()

            def theirs(step, carry, level=level, tile=tile, columns=columns):
                rows = pl.ds(pl.multiple_of(step * TILE, TILE), TILE)
                low_rows = pl.ds(pl.multiple_of(step * TILE + ANGLES, TILE), TILE)
                matrix = chosen[level, 1, rows, :]
                real = jnp.dot(matrix, taken[level, tile, 0], preferred_element_type=jnp.float32)
                imag = jnp.dot(matrix, taken[level, tile, 1], preferred_element_type=jnp.float32)
                cosine = cos_table[level, 1, rows, columns]
                sine = sin_table[level, 1, rows, columns]
                high = total[rows, columns] + (real * cosine - imag * sine)
                low = total[low_rows, columns] + (real * sine + imag * cosine)
                if level + 1 < LEVELS:
                    images[level + 1, rows, columns] = high.astype(jnp.bfloat16)
                    images[level + 1, low_rows, columns] = low.astype(jnp.bfloat16)
                else:
                    total[rows, columns] = high
                    total[low_rows, columns] = low
                return carry

            lax.fori_loop(0, ANGLES // TILE, theirs, 0)
            if level + 1 < LEVELS:
                send_rims(level + 1, left=tile == 0, right=tile == TILES - 1)
            else:
                for part in range(2):
                    pltpu.make_async_copy(
                        total.at[pl.ds(part * ANGLES, ANGLES), pl.ds(tile * TILE, TILE)],
                        out.at[part, :, pl.ds(tile * TILE, TILE)],
                        out_sem.at[part, tile],
                    ).start()

        for tile in ORDER:
            to_partner(tile).wait_send()

        @pl.when(block > 0)
        def _(level=level):
            to_left(level).wait_send()

        @pl.when(block < sources - 1)
        def _(level=level):
            to_right(level).wait_send()

    for tile in range(TILES):
        for part in range(2):
            pltpu.make_async_copy(
                total.at[pl.ds(part * ANGLES, ANGLES), pl.ds(tile * TILE, TILE)],
                out.at[part, :, pl.ds(tile * TILE, TILE)],
                out_sem.at[part, tile],
            ).wait()


def on_device(doppler, sources, echoes, fore_flag, band_offset, angle_interp, range_kernel, center_shift):
    pulses = echoes.shape[1]
    total_bins = echoes.shape[2]
    any_space = pl.BlockSpec(memory_space=pl.ANY)
    vmem = pl.BlockSpec(memory_space=pltpu.VMEM)
    smem = pl.BlockSpec(memory_space=pltpu.SMEM)
    bf16 = jnp.bfloat16
    return pl.pallas_call(
        functools.partial(kernel, sources, total_bins),
        out_shape=jax.ShapeDtypeStruct((2, ANGLES, BINS), jnp.float32),
        in_specs=[any_space, any_space, vmem, vmem, smem, smem, smem],
        out_specs=any_space,
        scratch_shapes=[
            pltpu.VMEM((sources, 2 * pulses, BINS), bf16),
            pltpu.VMEM((2 * ANGLES, 2 * PULSES), bf16),
            pltpu.VMEM((LEVELS, BINS + 2 * TILE, BINS), bf16),
            pltpu.VMEM((LEVELS, 2, ANGLES, HALF), bf16),
            pltpu.VMEM((LEVELS, 2 * ANGLES, BINS), bf16),
            pltpu.VMEM((LEVELS, 2 * ANGLES, TILE), bf16),
            pltpu.VMEM((LEVELS, 2 * ANGLES, TILE), bf16),
            pltpu.VMEM((LEVELS, TILES, 2, HALF, TILE), bf16),
            pltpu.VMEM((2, HALF, BINS), bf16),
            pltpu.VMEM((LEVELS, TILES, 2, HALF, TILE), bf16),
            pltpu.VMEM((2 * ANGLES, BINS), jnp.float32),
            pltpu.VMEM((LEVELS, 2, ANGLES, BINS), jnp.float32),
            pltpu.VMEM((LEVELS, 2, ANGLES, BINS), jnp.float32),
            pltpu.SemaphoreType.DMA((3,)),
            pltpu.SemaphoreType.DMA,
            pltpu.SemaphoreType.DMA((LEVELS, 2)),
            pltpu.SemaphoreType.DMA((LEVELS, 2)),
            pltpu.SemaphoreType.DMA((LEVELS, TILES)),
            pltpu.SemaphoreType.DMA((LEVELS, TILES)),
            pltpu.SemaphoreType.DMA((2, TILES)),
        ],
        compiler_params=pltpu.CompilerParams(collective_id=0, has_side_effects=True, vmem_limit_bytes=60 * 2**20),
    )(
        echoes.reshape(2 * pulses, total_bins),
        jnp.asarray(doppler),
        range_kernel,
        angle_interp,
        fore_flag[:, :, 0],
        band_offset[:, :, 0],
        center_shift,
    )


def solution(mesh):
    sources = mesh.shape["rng"]
    placed = (
        P(None, ("sub", "rng"), None),
        P(None, None, "rng"),
        P(None, None, "rng"),
        P(),
        P(),
        P(),
    )
    body = functools.partial(on_device, doppler_constant(sources), sources)
    return jax.shard_map(body, mesh=mesh, in_specs=placed, out_specs=P(None, "sub", "rng"), check_vma=False)
```

```python
import functools
import math

import jax
import jax.numpy as jnp
import ml_dtypes
import numpy as np
from jax import lax
from jax.experimental import pallas as pl
from jax.experimental.pallas import tpu as pltpu
from jax.sharding import PartitionSpec as P

ANGLES = 512
PULSES = 512
BINS = 512
TILE = 128
TILES = BINS // TILE
HALF = ANGLES // 2
BAND_HALF = 16
LEVELS = 3
MESH = pl.DeviceIdType.MESH
ORDERS = ((1, 2, 3, 0), (2, 1, 0, 3), (1, 2, 3, 0))


def doppler_constant(sources):
    angle = np.arange(ANGLES, dtype=np.int64)[:, None]
    pulse = np.arange(PULSES, dtype=np.int64)[None, :]
    cycles = (2 * angle + 1 - ANGLES) * pulse % (2 * ANGLES)
    phase = math.pi / ANGLES * cycles
    cosine = np.cos(phase) / math.sqrt(PULSES)
    sine = np.sin(phase) / math.sqrt(PULSES)
    whole = np.block([[cosine, sine], [-sine, cosine]])
    whole = whole.reshape(2 * ANGLES, 2, sources, PULSES // sources)
    return whole.transpose(0, 2, 1, 3).reshape(2 * ANGLES, 2 * PULSES).astype(ml_dtypes.bfloat16)


def kernel(
    sources,
    total_bins,
    echoes,
    doppler,
    kernels_far,
    interp_far,
    flags,
    offsets,
    shifts,
    out,
    turned,
    wide,
    kernels,
    interp,
    shifted,
    chosen,
    images,
    left_rim,
    right_rim,
    given,
    kept,
    taken,
    total,
    cos_table,
    sin_table,
    turn_sem,
    wide_sem,
    rim_send,
    rim_recv,
    pair_send,
    pair_recv,
    out_sem,
):
    group = lax.axis_index("sub")
    block = lax.axis_index("rng")
    partners = [jnp.bitwise_xor(group, 1 << level) for level in range(LEVELS)]

    barrier = pltpu.get_barrier_semaphore()

    def greet(step, carry):
        peer = lax.rem(block + step, sources)
        pl.semaphore_signal(barrier, inc=1, device_id=(group, peer), device_id_type=MESH)
        return carry

    for partner in partners[::-1]:
        pl.semaphore_signal(barrier, inc=1, device_id=(partner, block), device_id_type=MESH)
    lax.fori_loop(1, sources, greet, 0)
    loads = [
        pltpu.make_async_copy(source, target, wide_sem.at[place])
        for place, (source, target) in enumerate(((kernels_far, kernels), (interp_far, interp), (doppler, wide)))
    ]
    for load in loads:
        load.start()
    pl.semaphore_wait(barrier, sources - 1 + LEVELS)

    def turn(step, carry):
        peer = lax.rem(block + step, sources)
        pltpu.make_async_remote_copy(
            src_ref=echoes.at[:, pl.ds(pl.multiple_of(peer * BINS, BINS), BINS)],
            dst_ref=turned.at[block],
            send_sem=turn_sem.at[0],
            recv_sem=turn_sem.at[1],
            device_id=(group, peer),
            device_id_type=MESH,
        ).start()
        return carry

    lax.fori_loop(1, sources, turn, 0)
    stay = pltpu.make_async_copy(
        echoes.at[:, pl.ds(pl.multiple_of(block * BINS, BINS), BINS)], turned.at[block], turn_sem.at[2]
    )
    stay.start()

    loads[0].wait()
    loads[1].wait()
    for level in range(LEVELS):
        offset = offsets[level, 0, group]
        rows = lax.broadcasted_iota(jnp.int32, (TILE, BINS + 2 * BAND_HALF), 0)
        taps = lax.broadcasted_iota(jnp.int32, (TILE, BINS + 2 * BAND_HALF), 1)

        def shift(step, carry, level=level, offset=offset, rows=rows, taps=taps):
            start = pl.multiple_of(step * TILE, TILE)
            pick = jnp.where(rows + start == taps + (TILE - BAND_HALF + offset), 1.0, 0.0).astype(jnp.bfloat16)
            moved = jnp.dot(pick, kernels[level], preferred_element_type=jnp.float32)
            shifted[level, pl.ds(start, TILE), :] = moved.astype(jnp.bfloat16)
            return carry

        lax.fori_loop(0, TILES + 2, shift, 0)

        def choose(step, carry, level=level):
            rows = pl.ds(pl.multiple_of(step * TILE, TILE), TILE)
            zero = interp[level, 0, rows, :].astype(jnp.float32)
            one = interp[level, 1, rows, :].astype(jnp.float32)
            side = jnp.full((TILE, HALF), flags[level, 0, group], jnp.int32)
            chosen[level, 0, rows, :] = jnp.where(side == 1, one, zero).astype(jnp.bfloat16)
            chosen[level, 1, rows, :] = jnp.where(side == 1, zero, one).astype(jnp.bfloat16)
            return carry

        lax.fori_loop(0, ANGLES // TILE, choose, 0)

    rows_at_once = 32

    def tables(step, carry):
        first = pl.multiple_of(step * rows_at_once, rows_at_once)
        angle = lax.broadcasted_iota(jnp.int32, (rows_at_once, BINS), 0) + first
        angle_pos = (angle.astype(jnp.float32) + 0.5) / ANGLES - 0.5
        bins = lax.broadcasted_iota(jnp.int32, (rows_at_once, BINS), 1) + block * BINS
        range_pos = 1.0 + bins.astype(jnp.float32) / total_bins
        for level in range(LEVELS):
            for side, owner in enumerate((group, partners[level])):
                phase = math.pi * shifts[level, owner] * angle_pos * range_pos
                cos_table[level, side, pl.ds(first, rows_at_once), :] = jnp.cos(phase)
                sin_table[level, side, pl.ds(first, rows_at_once), :] = jnp.sin(phase)
        return carry

    lax.fori_loop(0, ANGLES // rows_at_once, tables, 0)

    @pl.when(block == 0)
    def _():
        for level in range(LEVELS):
            left_rim[level] = jnp.zeros((2 * ANGLES, TILE), jnp.bfloat16)

    @pl.when(block == sources - 1)
    def _():
        for level in range(LEVELS):
            right_rim[level] = jnp.zeros((2 * ANGLES, TILE), jnp.bfloat16)

    def to_left(level):
        return pltpu.make_async_remote_copy(
            src_ref=images.at[level, :, pl.ds(0, TILE)],
            dst_ref=right_rim.at[level],
            send_sem=rim_send.at[level, 0],
            recv_sem=rim_recv.at[level, 0],
            device_id=(group, block - 1),
            device_id_type=MESH,
        )

    def to_right(level):
        return pltpu.make_async_remote_copy(
            src_ref=images.at[level, :, pl.ds(BINS - TILE, TILE)],
            dst_ref=left_rim.at[level],
            send_sem=rim_send.at[level, 1],
            recv_sem=rim_recv.at[level, 1],
            device_id=(group, block + 1),
            device_id_type=MESH,
        )

    def send_rims(level, left=True, right=True):
        if left:

            @pl.when(block > 0)
            def _():
                to_left(level).start()

        if right:

            @pl.when(block < sources - 1)
            def _():
                to_right(level).start()

    loads[2].wait()
    stay.wait()
    others = turned.at[pl.ds(0, sources - 1)]
    pltpu.make_async_copy(others, others, turn_sem.at[1]).wait()

    def filtering(step, carry):
        start = pl.multiple_of(step * TILE, TILE)
        stack = turned[...].reshape(2 * PULSES, BINS)
        image = jnp.dot(wide[pl.ds(start, TILE), :], stack, preferred_element_type=jnp.float32)
        images[0, pl.ds(start, TILE), :] = image.astype(jnp.bfloat16)
        return carry

    lax.fori_loop(0, 2 * ANGLES // TILE, filtering, 0)
    send_rims(0)

    def to_partner(level, tile):
        return pltpu.make_async_remote_copy(
            src_ref=given.at[level, tile],
            dst_ref=taken.at[level, tile],
            send_sem=pair_send.at[level, tile],
            recv_sem=pair_recv.at[level, tile],
            device_id=(partners[level], block),
            device_id_type=MESH,
        )

    def resample(level, tile):
        if tile == 0:

            @pl.when(block > 0)
            def _():
                to_right(level).wait_recv()

        if tile == TILES - 1:

            @pl.when(block < sources - 1)
            def _():
                to_left(level).wait_recv()

        columns = slice(tile * TILE, tile * TILE + TILE)
        weights = shifted[level, tile * TILE : (tile + 3) * TILE, columns]
        flag = jnp.full((HALF, TILE), flags[level, 0, group], jnp.int32)
        for part in range(2):
            values = []
            for side in range(2):
                rows = slice(part * ANGLES + side * HALF, part * ANGLES + side * HALF + HALF)
                if tile == 0:
                    window = jnp.concatenate([left_rim[level, rows, :], images[level, rows, 0 : 2 * TILE]], axis=1)
                elif tile == TILES - 1:
                    window = jnp.concatenate([images[level, rows, BINS - 2 * TILE :], right_rim[level, rows, :]], axis=1)
                else:
                    window = images[level, rows, (tile - 1) * TILE : (tile + 2) * TILE]
                values.append(jnp.dot(window, weights, preferred_element_type=jnp.float32))
            given[level, tile, part] = jnp.where(flag == 1, values[0], values[1]).astype(jnp.bfloat16)
            kept[part, :, columns] = jnp.where(flag == 1, values[1], values[0]).astype(jnp.bfloat16)
        to_partner(level, tile).start()

    def to_out(part, tile):
        return pltpu.make_async_copy(
            total.at[pl.ds(part * ANGLES, ANGLES), pl.ds(tile * TILE, TILE)],
            out.at[part, :, pl.ds(tile * TILE, TILE)],
            out_sem.at[part, tile],
        )

    for tile in ORDERS[0]:
        resample(0, tile)
    for level in range(LEVELS):
        def own(step, carry, level=level):
            rows = pl.ds(pl.multiple_of(step * TILE, TILE), TILE)
            low_rows = pl.ds(pl.multiple_of(step * TILE + ANGLES, TILE), TILE)
            matrix = chosen[level, 0, rows, :]
            real = jnp.dot(matrix, kept[0], preferred_element_type=jnp.float32)
            imag = jnp.dot(matrix, kept[1], preferred_element_type=jnp.float32)
            cosine = cos_table[level, 0, rows, :]
            sine = sin_table[level, 0, rows, :]
            total[rows, :] = real * cosine - imag * sine
            total[low_rows, :] = real * sine + imag * cosine
            return carry

        lax.fori_loop(0, ANGLES // TILE, own, 0)

        for order, tile in enumerate(ORDERS[level]):
            columns = slice(tile * TILE, tile * TILE + TILE)
            to_partner(level, tile).wait_recv()

            def theirs(step, carry, level=level, tile=tile, columns=columns):
                rows = pl.ds(pl.multiple_of(step * TILE, TILE), TILE)
                low_rows = pl.ds(pl.multiple_of(step * TILE + ANGLES, TILE), TILE)
                matrix = chosen[level, 1, rows, :]
                real = jnp.dot(matrix, taken[level, tile, 0], preferred_element_type=jnp.float32)
                imag = jnp.dot(matrix, taken[level, tile, 1], preferred_element_type=jnp.float32)
                cosine = cos_table[level, 1, rows, columns]
                sine = sin_table[level, 1, rows, columns]
                high = total[rows, columns] + (real * cosine - imag * sine)
                low = total[low_rows, columns] + (real * sine + imag * cosine)
                if level + 1 < LEVELS:
                    images[level + 1, rows, columns] = high.astype(jnp.bfloat16)
                    images[level + 1, low_rows, columns] = low.astype(jnp.bfloat16)
                else:
                    total[rows, columns] = high
                    total[low_rows, columns] = low
                return carry

            lax.fori_loop(0, ANGLES // TILE, theirs, 0)
            if level + 1 < LEVELS:
                send_rims(level + 1, left=tile == 0, right=tile == TILES - 1)
                if order == 2:
                    resample(level + 1, ORDERS[level + 1][0])
                if order == 3:
                    for later in ORDERS[level + 1][1:]:
                        resample(level + 1, later)
            else:
                for part in range(2):
                    to_out(part, tile).start()

    for level in range(LEVELS):
        for tile in range(TILES):
            to_partner(level, tile).wait_send()

        @pl.when(block > 0)
        def _(level=level):
            to_left(level).wait_send()

        @pl.when(block < sources - 1)
        def _(level=level):
            to_right(level).wait_send()

    pltpu.make_async_copy(others, others, turn_sem.at[0]).wait()
    for tile in range(TILES):
        for part in range(2):
            to_out(part, tile).wait()


def on_device(doppler, sources, echoes, fore_flag, band_offset, angle_interp, range_kernel, center_shift):
    pulses = echoes.shape[1]
    total_bins = echoes.shape[2]
    any_space = pl.BlockSpec(memory_space=pl.ANY)
    smem = pl.BlockSpec(memory_space=pltpu.SMEM)
    bf16 = jnp.bfloat16
    return pl.pallas_call(
        functools.partial(kernel, sources, total_bins),
        out_shape=jax.ShapeDtypeStruct((2, ANGLES, BINS), jnp.float32),
        in_specs=[any_space, any_space, any_space, any_space, smem, smem, smem],
        out_specs=any_space,
        scratch_shapes=[
            pltpu.VMEM((sources, 2 * pulses, BINS), bf16),
            pltpu.VMEM((2 * ANGLES, 2 * PULSES), bf16),
            pltpu.VMEM(range_kernel.shape, bf16),
            pltpu.VMEM(angle_interp.shape, bf16),
            pltpu.VMEM((LEVELS, BINS + 2 * TILE, BINS), bf16),
            pltpu.VMEM((LEVELS, 2, ANGLES, HALF), bf16),
            pltpu.VMEM((LEVELS, 2 * ANGLES, BINS), bf16),
            pltpu.VMEM((LEVELS, 2 * ANGLES, TILE), bf16),
            pltpu.VMEM((LEVELS, 2 * ANGLES, TILE), bf16),
            pltpu.VMEM((LEVELS, TILES, 2, HALF, TILE), bf16),
            pltpu.VMEM((2, HALF, BINS), bf16),
            pltpu.VMEM((LEVELS, TILES, 2, HALF, TILE), bf16),
            pltpu.VMEM((2 * ANGLES, BINS), jnp.float32),
            pltpu.VMEM((LEVELS, 2, ANGLES, BINS), jnp.float32),
            pltpu.VMEM((LEVELS, 2, ANGLES, BINS), jnp.float32),
            pltpu.SemaphoreType.DMA((3,)),
            pltpu.SemaphoreType.DMA((3,)),
            pltpu.SemaphoreType.DMA((LEVELS, 2)),
            pltpu.SemaphoreType.DMA((LEVELS, 2)),
            pltpu.SemaphoreType.DMA((LEVELS, TILES)),
            pltpu.SemaphoreType.DMA((LEVELS, TILES)),
            pltpu.SemaphoreType.DMA((2, TILES)),
        ],
        compiler_params=pltpu.CompilerParams(collective_id=0, has_side_effects=True, vmem_limit_bytes=60 * 2**20),
    )(
        echoes.reshape(2 * pulses, total_bins),
        jnp.asarray(doppler),
        range_kernel,
        angle_interp,
        fore_flag.transpose(0, 2, 1),
        band_offset.transpose(0, 2, 1),
        center_shift,
    )


def solution(mesh):
    sources = mesh.shape["rng"]
    placed = (
        P(None, ("sub", "rng"), None),
        P(None, None, "rng"),
        P(None, None, "rng"),
        P(),
        P(),
        P(),
    )
    body = functools.partial(on_device, doppler_constant(sources), sources)
    return jax.shard_map(body, mesh=mesh, in_specs=placed, out_specs=P(None, "sub", "rng"), check_vma=False)
```

```python
import functools
import math

import jax
import jax.numpy as jnp
import ml_dtypes
import numpy as np
from jax import lax
from jax.experimental import pallas as pl
from jax.experimental.pallas import tpu as pltpu
from jax.sharding import PartitionSpec as P

ANGLES = 512
PULSES = 512
BINS = 512
TILE = 128
TILES = BINS // TILE
HALF = ANGLES // 2
BAND_HALF = 16
LEVELS = 3
MESH = pl.DeviceIdType.MESH
ORDERS = ((1, 2, 3, 0), (2, 1, 0, 3), (1, 2, 3, 0))


def doppler_constant(sources):
    angle = np.arange(ANGLES, dtype=np.int64)[:, None]
    pulse = np.arange(PULSES, dtype=np.int64)[None, :]
    cycles = (2 * angle + 1 - ANGLES) * pulse % (2 * ANGLES)
    phase = math.pi / ANGLES * cycles
    cosine = np.cos(phase) / math.sqrt(PULSES)
    sine = np.sin(phase) / math.sqrt(PULSES)
    whole = np.block([[cosine, sine], [-sine, cosine]])
    whole = whole.reshape(2 * ANGLES, 2, sources, PULSES // sources)
    return whole.transpose(0, 2, 1, 3).reshape(2 * ANGLES, 2 * PULSES).astype(ml_dtypes.bfloat16)


def kernel(
    sources,
    total_bins,
    echoes,
    doppler,
    kernels_far,
    interp_far,
    flags,
    offsets,
    shifts,
    out,
    turned,
    turned_last,
    wide,
    kernels,
    interp,
    shifted,
    chosen,
    images,
    left_rim,
    right_rim,
    given,
    kept,
    taken,
    total,
    cos_table,
    sin_table,
    turn_sem,
    wide_sem,
    rim_send,
    rim_recv,
    pair_send,
    pair_recv,
    out_sem,
):
    group = lax.axis_index("sub")
    block = lax.axis_index("rng")
    partners = [jnp.bitwise_xor(group, 1 << level) for level in range(LEVELS)]

    barrier = pltpu.get_barrier_semaphore()

    def greet(step, carry):
        peer = lax.rem(block + step, sources)
        pl.semaphore_signal(barrier, inc=1, device_id=(group, peer), device_id_type=MESH)
        return carry

    for partner in partners[::-1]:
        pl.semaphore_signal(barrier, inc=1, device_id=(partner, block), device_id_type=MESH)
    lax.fori_loop(1, sources, greet, 0)
    loads = [
        pltpu.make_async_copy(source, target, wide_sem.at[place])
        for place, (source, target) in enumerate(((kernels_far, kernels), (interp_far, interp), (doppler, wide)))
    ]
    for load in loads:
        load.start()
    pl.semaphore_wait(barrier, sources - 1 + LEVELS)

    rounds = ((turned, 0, BINS - TILE), (turned_last, BINS - TILE, TILE))

    def columns_of(owner, start, width):
        return pl.ds(pl.multiple_of(owner * BINS + start, TILE), width)

    for place, (target, start, width) in enumerate(rounds):

        def turn(step, carry, place=place, target=target, start=start, width=width):
            peer = lax.rem(block + step, sources)
            pltpu.make_async_remote_copy(
                src_ref=echoes.at[:, columns_of(peer, start, width)],
                dst_ref=target.at[block],
                send_sem=turn_sem.at[place, 0],
                recv_sem=turn_sem.at[place, 1],
                device_id=(group, peer),
                device_id_type=MESH,
            ).start()
            return carry

        lax.fori_loop(1, sources, turn, 0)

    def stay(place):
        target, start, width = rounds[place]
        return pltpu.make_async_copy(
            echoes.at[:, columns_of(block, start, width)], target.at[block], turn_sem.at[place, 2]
        )

    stay(0).start()
    stay(1).start()

    loads[0].wait()
    loads[1].wait()
    for level in range(LEVELS):
        offset = offsets[level, 0, group]
        rows = lax.broadcasted_iota(jnp.int32, (TILE, BINS + 2 * BAND_HALF), 0)
        taps = lax.broadcasted_iota(jnp.int32, (TILE, BINS + 2 * BAND_HALF), 1)

        def shift(step, carry, level=level, offset=offset, rows=rows, taps=taps):
            start = pl.multiple_of(step * TILE, TILE)
            pick = jnp.where(rows + start == taps + (TILE - BAND_HALF + offset), 1.0, 0.0).astype(jnp.bfloat16)
            moved = jnp.dot(pick, kernels[level], preferred_element_type=jnp.float32)
            shifted[level, pl.ds(start, TILE), :] = moved.astype(jnp.bfloat16)
            return carry

        lax.fori_loop(0, TILES + 2, shift, 0)

        def choose(step, carry, level=level):
            rows = pl.ds(pl.multiple_of(step * TILE, TILE), TILE)
            zero = interp[level, 0, rows, :].astype(jnp.float32)
            one = interp[level, 1, rows, :].astype(jnp.float32)
            side = jnp.full((TILE, HALF), flags[level, 0, group], jnp.int32)
            chosen[level, 0, rows, :] = jnp.where(side == 1, one, zero).astype(jnp.bfloat16)
            chosen[level, 1, rows, :] = jnp.where(side == 1, zero, one).astype(jnp.bfloat16)
            return carry

        lax.fori_loop(0, ANGLES // TILE, choose, 0)

    rows_at_once = 32

    def tables(step, carry, levels):
        first = pl.multiple_of(step * rows_at_once, rows_at_once)
        angle = lax.broadcasted_iota(jnp.int32, (rows_at_once, BINS), 0) + first
        angle_pos = (angle.astype(jnp.float32) + 0.5) / ANGLES - 0.5
        bins = lax.broadcasted_iota(jnp.int32, (rows_at_once, BINS), 1) + block * BINS
        range_pos = 1.0 + bins.astype(jnp.float32) / total_bins
        for level in levels:
            for side, owner in enumerate((group, partners[level])):
                phase = math.pi * shifts[level, owner] * angle_pos * range_pos
                cos_table[level, side, pl.ds(first, rows_at_once), :] = jnp.cos(phase)
                sin_table[level, side, pl.ds(first, rows_at_once), :] = jnp.sin(phase)
        return carry

    def make_tables(*levels):
        lax.fori_loop(0, ANGLES // rows_at_once, functools.partial(tables, levels=levels), 0)

    make_tables(0, 1)

    @pl.when(block == 0)
    def _():
        for level in range(LEVELS):
            left_rim[level] = jnp.zeros((2 * ANGLES, TILE), jnp.bfloat16)

    @pl.when(block == sources - 1)
    def _():
        for level in range(LEVELS):
            right_rim[level] = jnp.zeros((2 * ANGLES, TILE), jnp.bfloat16)

    def to_left(level):
        return pltpu.make_async_remote_copy(
            src_ref=images.at[level, :, pl.ds(0, TILE)],
            dst_ref=right_rim.at[level],
            send_sem=rim_send.at[level, 0],
            recv_sem=rim_recv.at[level, 0],
            device_id=(group, block - 1),
            device_id_type=MESH,
        )

    def to_right(level):
        return pltpu.make_async_remote_copy(
            src_ref=images.at[level, :, pl.ds(BINS - TILE, TILE)],
            dst_ref=left_rim.at[level],
            send_sem=rim_send.at[level, 1],
            recv_sem=rim_recv.at[level, 1],
            device_id=(group, block + 1),
            device_id_type=MESH,
        )

    def send_rims(level, left=True, right=True):
        if left:

            @pl.when(block > 0)
            def _():
                to_left(level).start()

        if right:

            @pl.when(block < sources - 1)
            def _():
                to_right(level).start()

    loads[2].wait()

    def others(place):
        target = rounds[place][0].at[pl.ds(0, sources - 1)]
        return [pltpu.make_async_copy(target, target, turn_sem.at[place, side]) for side in range(2)]

    def filter_round(place):
        target, first, width = rounds[place]
        stay(place).wait()
        others(place)[1].wait()

        def filtering(step, carry):
            start = pl.multiple_of(step * TILE, TILE)
            stack = target[...].reshape(2 * PULSES, width)
            image = jnp.dot(wide[pl.ds(start, TILE), :], stack, preferred_element_type=jnp.float32)
            images[0, pl.ds(start, TILE), first : first + width] = image.astype(jnp.bfloat16)
            return carry

        lax.fori_loop(0, 2 * ANGLES // TILE, filtering, 0)

    def to_partner(level, tile):
        return pltpu.make_async_remote_copy(
            src_ref=given.at[level, tile],
            dst_ref=taken.at[level, tile],
            send_sem=pair_send.at[level, tile],
            recv_sem=pair_recv.at[level, tile],
            device_id=(partners[level], block),
            device_id_type=MESH,
        )

    def resample(level, tile):
        if tile == 0:

            @pl.when(block > 0)
            def _():
                to_right(level).wait_recv()

        if tile == TILES - 1:

            @pl.when(block < sources - 1)
            def _():
                to_left(level).wait_recv()

        columns = slice(tile * TILE, tile * TILE + TILE)
        weights = shifted[level, tile * TILE : (tile + 3) * TILE, columns]
        flag = jnp.full((HALF, TILE), flags[level, 0, group], jnp.int32)
        for part in range(2):
            values = []
            for side in range(2):
                rows = slice(part * ANGLES + side * HALF, part * ANGLES + side * HALF + HALF)
                if tile == 0:
                    window = jnp.concatenate([left_rim[level, rows, :], images[level, rows, 0 : 2 * TILE]], axis=1)
                elif tile == TILES - 1:
                    window = jnp.concatenate([images[level, rows, BINS - 2 * TILE :], right_rim[level, rows, :]], axis=1)
                else:
                    window = images[level, rows, (tile - 1) * TILE : (tile + 2) * TILE]
                values.append(jnp.dot(window, weights, preferred_element_type=jnp.float32))
            given[level, tile, part] = jnp.where(flag == 1, values[0], values[1]).astype(jnp.bfloat16)
            kept[part, :, columns] = jnp.where(flag == 1, values[1], values[0]).astype(jnp.bfloat16)
        to_partner(level, tile).start()

    def to_out(part, tile):
        return pltpu.make_async_copy(
            total.at[pl.ds(part * ANGLES, ANGLES), pl.ds(tile * TILE, TILE)],
            out.at[part, :, pl.ds(tile * TILE, TILE)],
            out_sem.at[part, tile],
        )

    filter_round(0)
    send_rims(0, right=False)
    resample(0, ORDERS[0][0])
    filter_round(1)
    send_rims(0, left=False)
    for tile in ORDERS[0][1:]:
        resample(0, tile)
    for level in range(LEVELS):
        if level == LEVELS - 1:
            make_tables(level)

        def own(step, carry, level=level):
            rows = pl.ds(pl.multiple_of(step * TILE, TILE), TILE)
            low_rows = pl.ds(pl.multiple_of(step * TILE + ANGLES, TILE), TILE)
            matrix = chosen[level, 0, rows, :]
            real = jnp.dot(matrix, kept[0], preferred_element_type=jnp.float32)
            imag = jnp.dot(matrix, kept[1], preferred_element_type=jnp.float32)
            cosine = cos_table[level, 0, rows, :]
            sine = sin_table[level, 0, rows, :]
            total[rows, :] = real * cosine - imag * sine
            total[low_rows, :] = real * sine + imag * cosine
            return carry

        lax.fori_loop(0, ANGLES // TILE, own, 0)

        for order, tile in enumerate(ORDERS[level]):
            columns = slice(tile * TILE, tile * TILE + TILE)
            to_partner(level, tile).wait_recv()

            def theirs(step, carry, level=level, tile=tile, columns=columns):
                rows = pl.ds(pl.multiple_of(step * TILE, TILE), TILE)
                low_rows = pl.ds(pl.multiple_of(step * TILE + ANGLES, TILE), TILE)
                matrix = chosen[level, 1, rows, :]
                real = jnp.dot(matrix, taken[level, tile, 0], preferred_element_type=jnp.float32)
                imag = jnp.dot(matrix, taken[level, tile, 1], preferred_element_type=jnp.float32)
                cosine = cos_table[level, 1, rows, columns]
                sine = sin_table[level, 1, rows, columns]
                high = total[rows, columns] + (real * cosine - imag * sine)
                low = total[low_rows, columns] + (real * sine + imag * cosine)
                if level + 1 < LEVELS:
                    images[level + 1, rows, columns] = high.astype(jnp.bfloat16)
                    images[level + 1, low_rows, columns] = low.astype(jnp.bfloat16)
                else:
                    total[rows, columns] = high
                    total[low_rows, columns] = low
                return carry

            lax.fori_loop(0, ANGLES // TILE, theirs, 0)
            if level + 1 < LEVELS:
                send_rims(level + 1, left=tile == 0, right=tile == TILES - 1)
                if order == 2:
                    resample(level + 1, ORDERS[level + 1][0])
                if order == 3:
                    for later in ORDERS[level + 1][1:]:
                        resample(level + 1, later)
            else:
                for part in range(2):
                    to_out(part, tile).start()

    for level in range(LEVELS):
        for tile in range(TILES):
            to_partner(level, tile).wait_send()

        @pl.when(block > 0)
        def _(level=level):
            to_left(level).wait_send()

        @pl.when(block < sources - 1)
        def _(level=level):
            to_right(level).wait_send()

    for place in range(2):
        others(place)[0].wait()
    for tile in range(TILES):
        for part in range(2):
            to_out(part, tile).wait()


def on_device(doppler, sources, echoes, fore_flag, band_offset, angle_interp, range_kernel, center_shift):
    pulses = echoes.shape[1]
    total_bins = echoes.shape[2]
    any_space = pl.BlockSpec(memory_space=pl.ANY)
    smem = pl.BlockSpec(memory_space=pltpu.SMEM)
    bf16 = jnp.bfloat16
    return pl.pallas_call(
        functools.partial(kernel, sources, total_bins),
        out_shape=jax.ShapeDtypeStruct((2, ANGLES, BINS), jnp.float32),
        in_specs=[any_space, any_space, any_space, any_space, smem, smem, smem],
        out_specs=any_space,
        scratch_shapes=[
            pltpu.VMEM((sources, 2 * pulses, BINS - TILE), bf16),
            pltpu.VMEM((sources, 2 * pulses, TILE), bf16),
            pltpu.VMEM((2 * ANGLES, 2 * PULSES), bf16),
            pltpu.VMEM(range_kernel.shape, bf16),
            pltpu.VMEM(angle_interp.shape, bf16),
            pltpu.VMEM((LEVELS, BINS + 2 * TILE, BINS), bf16),
            pltpu.VMEM((LEVELS, 2, ANGLES, HALF), bf16),
            pltpu.VMEM((LEVELS, 2 * ANGLES, BINS), bf16),
            pltpu.VMEM((LEVELS, 2 * ANGLES, TILE), bf16),
            pltpu.VMEM((LEVELS, 2 * ANGLES, TILE), bf16),
            pltpu.VMEM((LEVELS, TILES, 2, HALF, TILE), bf16),
            pltpu.VMEM((2, HALF, BINS), bf16),
            pltpu.VMEM((LEVELS, TILES, 2, HALF, TILE), bf16),
            pltpu.VMEM((2 * ANGLES, BINS), jnp.float32),
            pltpu.VMEM((LEVELS, 2, ANGLES, BINS), jnp.float32),
            pltpu.VMEM((LEVELS, 2, ANGLES, BINS), jnp.float32),
            pltpu.SemaphoreType.DMA((2, 3)),
            pltpu.SemaphoreType.DMA((3,)),
            pltpu.SemaphoreType.DMA((LEVELS, 2)),
            pltpu.SemaphoreType.DMA((LEVELS, 2)),
            pltpu.SemaphoreType.DMA((LEVELS, TILES)),
            pltpu.SemaphoreType.DMA((LEVELS, TILES)),
            pltpu.SemaphoreType.DMA((2, TILES)),
        ],
        compiler_params=pltpu.CompilerParams(collective_id=0, has_side_effects=True, vmem_limit_bytes=60 * 2**20),
    )(
        echoes.reshape(2 * pulses, total_bins),
        jnp.asarray(doppler),
        range_kernel,
        angle_interp,
        fore_flag.transpose(0, 2, 1),
        band_offset.transpose(0, 2, 1),
        center_shift,
    )


def solution(mesh):
    sources = mesh.shape["rng"]
    placed = (
        P(None, ("sub", "rng"), None),
        P(None, None, "rng"),
        P(None, None, "rng"),
        P(),
        P(),
        P(),
    )
    body = functools.partial(on_device, doppler_constant(sources), sources)
    return jax.shard_map(body, mesh=mesh, in_specs=placed, out_specs=P(None, "sub", "rng"), check_vma=False)
```

```python
import functools
import math

import jax
import jax.numpy as jnp
import ml_dtypes
import numpy as np
from jax import lax
from jax.experimental import pallas as pl
from jax.experimental.pallas import tpu as pltpu
from jax.sharding import PartitionSpec as P

ANGLES = 512
PULSES = 512
BINS = 512
TILE = 128
TILES = BINS // TILE
HALF = ANGLES // 2
BAND_HALF = 16
LEVELS = 3
MESH = pl.DeviceIdType.MESH
ORDERS = ((1, 2, 3, 0), (2, 1, 0, 3), (1, 2, 3, 0))


def doppler_constant(sources):
    angle = np.arange(ANGLES, dtype=np.int64)[:, None]
    pulse = np.arange(PULSES, dtype=np.int64)[None, :]
    cycles = (2 * angle + 1 - ANGLES) * pulse % (2 * ANGLES)
    phase = math.pi / ANGLES * cycles
    cosine = np.cos(phase) / math.sqrt(PULSES)
    sine = np.sin(phase) / math.sqrt(PULSES)
    whole = np.block([[cosine, sine], [-sine, cosine]])
    whole = whole.reshape(2 * ANGLES, 2, sources, PULSES // sources)
    return whole.transpose(0, 2, 1, 3).reshape(2 * ANGLES, 2 * PULSES).astype(ml_dtypes.bfloat16)


def kernel(
    sources,
    total_bins,
    echoes,
    doppler,
    kernels_far,
    interp_far,
    flags,
    offsets,
    shifts,
    out,
    turned,
    wide,
    kernels,
    interp,
    shifted,
    chosen,
    images,
    left_rim,
    right_rim,
    given,
    kept,
    taken,
    total,
    cos_table,
    sin_table,
    turn_sem,
    wide_sem,
    rim_send,
    rim_recv,
    pair_send,
    pair_recv,
    out_sem,
):
    group = lax.axis_index("sub")
    block = lax.axis_index("rng")
    partners = [jnp.bitwise_xor(group, 1 << level) for level in range(LEVELS)]

    barrier = pltpu.get_barrier_semaphore()

    def greet(step, carry):
        peer = lax.rem(block + step, sources)
        pl.semaphore_signal(barrier, inc=1, device_id=(group, peer), device_id_type=MESH)
        return carry

    for partner in partners[::-1]:
        pl.semaphore_signal(barrier, inc=1, device_id=(partner, block), device_id_type=MESH)
    lax.fori_loop(1, sources, greet, 0)
    loads = [
        pltpu.make_async_copy(source, target, wide_sem.at[place])
        for place, (source, target) in enumerate(((kernels_far, kernels), (interp_far, interp), (doppler, wide)))
    ]
    for load in loads:
        load.start()
    pl.semaphore_wait(barrier, sources - 1 + LEVELS)

    def turn(step, carry):
        peer = lax.rem(block + step, sources)
        pltpu.make_async_remote_copy(
            src_ref=echoes.at[:, pl.ds(pl.multiple_of(peer * BINS, BINS), BINS)],
            dst_ref=turned.at[block],
            send_sem=turn_sem.at[0],
            recv_sem=turn_sem.at[1],
            device_id=(group, peer),
            device_id_type=MESH,
        ).start()
        return carry

    lax.fori_loop(1, sources, turn, 0)
    stay = pltpu.make_async_copy(
        echoes.at[:, pl.ds(pl.multiple_of(block * BINS, BINS), BINS)], turned.at[block], turn_sem.at[2]
    )
    stay.start()

    loads[0].wait()
    loads[1].wait()
    for level in range(LEVELS):
        offset = offsets[level, 0, group]
        rows = lax.broadcasted_iota(jnp.int32, (TILE, BINS + 2 * BAND_HALF), 0)
        taps = lax.broadcasted_iota(jnp.int32, (TILE, BINS + 2 * BAND_HALF), 1)

        def shift(step, carry, level=level, offset=offset, rows=rows, taps=taps):
            start = pl.multiple_of(step * TILE, TILE)
            pick = jnp.where(rows + start == taps + (TILE - BAND_HALF + offset), 1.0, 0.0).astype(jnp.bfloat16)
            moved = jnp.dot(pick, kernels[level], preferred_element_type=jnp.float32)
            shifted[level, pl.ds(start, TILE), :] = moved.astype(jnp.bfloat16)
            return carry

        lax.fori_loop(0, TILES + 2, shift, 0)

        def choose(step, carry, level=level):
            rows = pl.ds(pl.multiple_of(step * TILE, TILE), TILE)
            zero = interp[level, 0, rows, :].astype(jnp.float32)
            one = interp[level, 1, rows, :].astype(jnp.float32)
            side = jnp.full((TILE, HALF), flags[level, 0, group], jnp.int32)
            chosen[level, 0, rows, :] = jnp.where(side == 1, one, zero).astype(jnp.bfloat16)
            chosen[level, 1, rows, :] = jnp.where(side == 1, zero, one).astype(jnp.bfloat16)
            return carry

        lax.fori_loop(0, ANGLES // TILE, choose, 0)

    rows_at_once = 32

    def tables(step, carry):
        first = pl.multiple_of(step * rows_at_once, rows_at_once)
        angle = lax.broadcasted_iota(jnp.int32, (rows_at_once, BINS), 0) + first
        angle_pos = (angle.astype(jnp.float32) + 0.5) / ANGLES - 0.5
        bins = lax.broadcasted_iota(jnp.int32, (rows_at_once, BINS), 1) + block * BINS
        range_pos = 1.0 + bins.astype(jnp.float32) / total_bins
        for level in range(LEVELS):
            for side, owner in enumerate((group, partners[level])):
                phase = math.pi * shifts[level, owner] * angle_pos * range_pos
                cos_table[level, side, pl.ds(first, rows_at_once), :] = jnp.cos(phase)
                sin_table[level, side, pl.ds(first, rows_at_once), :] = jnp.sin(phase)
        return carry

    lax.fori_loop(0, ANGLES // rows_at_once, tables, 0)

    @pl.when(block == 0)
    def _():
        for level in range(LEVELS):
            left_rim[level] = jnp.zeros((2 * ANGLES, TILE), jnp.bfloat16)

    @pl.when(block == sources - 1)
    def _():
        for level in range(LEVELS):
            right_rim[level] = jnp.zeros((2 * ANGLES, TILE), jnp.bfloat16)

    def to_left(level):
        return pltpu.make_async_remote_copy(
            src_ref=images.at[level, :, pl.ds(0, TILE)],
            dst_ref=right_rim.at[level],
            send_sem=rim_send.at[level, 0],
            recv_sem=rim_recv.at[level, 0],
            device_id=(group, block - 1),
            device_id_type=MESH,
        )

    def to_right(level):
        return pltpu.make_async_remote_copy(
            src_ref=images.at[level, :, pl.ds(BINS - TILE, TILE)],
            dst_ref=left_rim.at[level],
            send_sem=rim_send.at[level, 1],
            recv_sem=rim_recv.at[level, 1],
            device_id=(group, block + 1),
            device_id_type=MESH,
        )

    def send_rims(level, left=True, right=True):
        if left:

            @pl.when(block > 0)
            def _():
                to_left(level).start()

        if right:

            @pl.when(block < sources - 1)
            def _():
                to_right(level).start()

    loads[2].wait()
    stay.wait()
    others = turned.at[pl.ds(0, sources - 1)]
    pltpu.make_async_copy(others, others, turn_sem.at[1]).wait()

    for part in range(2):
        rows = slice(part * ANGLES, part * ANGLES + ANGLES)
        image = jnp.dot(wide[rows, :], turned[...].reshape(2 * PULSES, BINS), preferred_element_type=jnp.float32)
        images[0, rows, :] = image.astype(jnp.bfloat16)
    send_rims(0)

    def to_partner(level, tile):
        return pltpu.make_async_remote_copy(
            src_ref=given.at[level, tile],
            dst_ref=taken.at[level, tile],
            send_sem=pair_send.at[level, tile],
            recv_sem=pair_recv.at[level, tile],
            device_id=(partners[level], block),
            device_id_type=MESH,
        )

    def resample(level, tile):
        if tile == 0:

            @pl.when(block > 0)
            def _():
                to_right(level).wait_recv()

        if tile == TILES - 1:

            @pl.when(block < sources - 1)
            def _():
                to_left(level).wait_recv()

        columns = slice(tile * TILE, tile * TILE + TILE)
        weights = shifted[level, tile * TILE : (tile + 3) * TILE, columns]
        flag = jnp.full((HALF, TILE), flags[level, 0, group], jnp.int32)
        for part in range(2):
            rows = slice(part * ANGLES, part * ANGLES + ANGLES)
            if tile == 0:
                window = jnp.concatenate([left_rim[level, rows, :], images[level, rows, 0 : 2 * TILE]], axis=1)
            elif tile == TILES - 1:
                window = jnp.concatenate([images[level, rows, BINS - 2 * TILE :], right_rim[level, rows, :]], axis=1)
            else:
                window = images[level, rows, (tile - 1) * TILE : (tile + 2) * TILE]
            both = jnp.dot(window, weights, preferred_element_type=jnp.float32)
            values = (both[0:HALF], both[HALF:ANGLES])
            given[level, tile, part] = jnp.where(flag == 1, values[0], values[1]).astype(jnp.bfloat16)
            kept[part, :, columns] = jnp.where(flag == 1, values[1], values[0]).astype(jnp.bfloat16)
        to_partner(level, tile).start()

    def to_out(part, tile):
        return pltpu.make_async_copy(
            total.at[pl.ds(part * ANGLES, ANGLES), pl.ds(tile * TILE, TILE)],
            out.at[part, :, pl.ds(tile * TILE, TILE)],
            out_sem.at[part, tile],
        )

    for tile in ORDERS[0]:
        resample(0, tile)
    for level in range(LEVELS):
        def own(step, carry, level=level):
            rows = pl.ds(pl.multiple_of(step * TILE, TILE), TILE)
            low_rows = pl.ds(pl.multiple_of(step * TILE + ANGLES, TILE), TILE)
            matrix = chosen[level, 0, rows, :]
            real = jnp.dot(matrix, kept[0], preferred_element_type=jnp.float32)
            imag = jnp.dot(matrix, kept[1], preferred_element_type=jnp.float32)
            cosine = cos_table[level, 0, rows, :]
            sine = sin_table[level, 0, rows, :]
            total[rows, :] = real * cosine - imag * sine
            total[low_rows, :] = real * sine + imag * cosine
            return carry

        lax.fori_loop(0, ANGLES // TILE, own, 0)

        for order, tile in enumerate(ORDERS[level]):
            columns = slice(tile * TILE, tile * TILE + TILE)
            to_partner(level, tile).wait_recv()

            matrix = chosen[level, 1]
            real = jnp.dot(matrix, taken[level, tile, 0], preferred_element_type=jnp.float32)
            imag = jnp.dot(matrix, taken[level, tile, 1], preferred_element_type=jnp.float32)
            cosine = cos_table[level, 1, :, columns]
            sine = sin_table[level, 1, :, columns]
            high = total[0:ANGLES, columns] + (real * cosine - imag * sine)
            low = total[ANGLES : 2 * ANGLES, columns] + (real * sine + imag * cosine)
            if level + 1 < LEVELS:
                images[level + 1, 0:ANGLES, columns] = high.astype(jnp.bfloat16)
                images[level + 1, ANGLES : 2 * ANGLES, columns] = low.astype(jnp.bfloat16)
            else:
                total[0:ANGLES, columns] = high
                total[ANGLES : 2 * ANGLES, columns] = low

            if level + 1 < LEVELS:
                send_rims(level + 1, left=tile == 0, right=tile == TILES - 1)
                if order == 2:
                    resample(level + 1, ORDERS[level + 1][0])
                if order == 3:
                    for later in ORDERS[level + 1][1:]:
                        resample(level + 1, later)
            else:
                for part in range(2):
                    to_out(part, tile).start()

    for level in range(LEVELS):
        for tile in range(TILES):
            to_partner(level, tile).wait_send()

        @pl.when(block > 0)
        def _(level=level):
            to_left(level).wait_send()

        @pl.when(block < sources - 1)
        def _(level=level):
            to_right(level).wait_send()

    pltpu.make_async_copy(others, others, turn_sem.at[0]).wait()
    for tile in range(TILES):
        for part in range(2):
            to_out(part, tile).wait()


def on_device(doppler, sources, echoes, fore_flag, band_offset, angle_interp, range_kernel, center_shift):
    pulses = echoes.shape[1]
    total_bins = echoes.shape[2]
    any_space = pl.BlockSpec(memory_space=pl.ANY)
    smem = pl.BlockSpec(memory_space=pltpu.SMEM)
    bf16 = jnp.bfloat16
    return pl.pallas_call(
        functools.partial(kernel, sources, total_bins),
        out_shape=jax.ShapeDtypeStruct((2, ANGLES, BINS), jnp.float32),
        in_specs=[any_space, any_space, any_space, any_space, smem, smem, smem],
        out_specs=any_space,
        scratch_shapes=[
            pltpu.VMEM((sources, 2 * pulses, BINS), bf16),
            pltpu.VMEM((2 * ANGLES, 2 * PULSES), bf16),
            pltpu.VMEM(range_kernel.shape, bf16),
            pltpu.VMEM(angle_interp.shape, bf16),
            pltpu.VMEM((LEVELS, BINS + 2 * TILE, BINS), bf16),
            pltpu.VMEM((LEVELS, 2, ANGLES, HALF), bf16),
            pltpu.VMEM((LEVELS, 2 * ANGLES, BINS), bf16),
            pltpu.VMEM((LEVELS, 2 * ANGLES, TILE), bf16),
            pltpu.VMEM((LEVELS, 2 * ANGLES, TILE), bf16),
            pltpu.VMEM((LEVELS, TILES, 2, HALF, TILE), bf16),
            pltpu.VMEM((2, HALF, BINS), bf16),
            pltpu.VMEM((LEVELS, TILES, 2, HALF, TILE), bf16),
            pltpu.VMEM((2 * ANGLES, BINS), jnp.float32),
            pltpu.VMEM((LEVELS, 2, ANGLES, BINS), jnp.float32),
            pltpu.VMEM((LEVELS, 2, ANGLES, BINS), jnp.float32),
            pltpu.SemaphoreType.DMA((3,)),
            pltpu.SemaphoreType.DMA((3,)),
            pltpu.SemaphoreType.DMA((LEVELS, 2)),
            pltpu.SemaphoreType.DMA((LEVELS, 2)),
            pltpu.SemaphoreType.DMA((LEVELS, TILES)),
            pltpu.SemaphoreType.DMA((LEVELS, TILES)),
            pltpu.SemaphoreType.DMA((2, TILES)),
        ],
        compiler_params=pltpu.CompilerParams(collective_id=0, has_side_effects=True, vmem_limit_bytes=60 * 2**20),
    )(
        echoes.reshape(2 * pulses, total_bins),
        jnp.asarray(doppler),
        range_kernel,
        angle_interp,
        fore_flag.transpose(0, 2, 1),
        band_offset.transpose(0, 2, 1),
        center_shift,
    )


def solution(mesh):
    sources = mesh.shape["rng"]
    placed = (
        P(None, ("sub", "rng"), None),
        P(None, None, "rng"),
        P(None, None, "rng"),
        P(),
        P(),
        P(),
    )
    body = functools.partial(on_device, doppler_constant(sources), sources)
    return jax.shard_map(body, mesh=mesh, in_specs=placed, out_specs=P(None, "sub", "rng"), check_vma=False)
```

```python
import functools
import math

import jax
import jax.numpy as jnp
import ml_dtypes
import numpy as np
from jax import lax
from jax.experimental import pallas as pl
from jax.experimental.pallas import tpu as pltpu
from jax.sharding import PartitionSpec as P

ANGLES = 512
PULSES = 512
BINS = 512
TILE = 128
TILES = BINS // TILE
HALF = ANGLES // 2
BAND_HALF = 16
LEVELS = 3
MESH = pl.DeviceIdType.MESH
ORDERS = ((1, 2, 3, 0), (2, 1, 0, 3), (1, 2, 3, 0))


def doppler_constant(sources):
    angle = np.arange(ANGLES, dtype=np.int64)[:, None]
    pulse = np.arange(PULSES, dtype=np.int64)[None, :]
    cycles = (2 * angle + 1 - ANGLES) * pulse % (2 * ANGLES)
    phase = math.pi / ANGLES * cycles
    cosine = np.cos(phase) / math.sqrt(PULSES)
    sine = np.sin(phase) / math.sqrt(PULSES)
    whole = np.block([[cosine, sine], [-sine, cosine]])
    whole = whole.reshape(2 * ANGLES, 2, sources, PULSES // sources)
    return whole.transpose(0, 2, 1, 3).reshape(2 * ANGLES, 2 * PULSES).astype(ml_dtypes.bfloat16)


def kernel(
    sources,
    total_bins,
    echoes,
    doppler,
    kernels_far,
    interp_far,
    flags,
    offsets,
    shifts,
    out,
    turned,
    wide,
    kernels,
    interp,
    shifted,
    chosen,
    images,
    left_rim,
    right_rim,
    given,
    kept,
    taken,
    total,
    cos_table,
    sin_table,
    turn_sem,
    wide_sem,
    rim_send,
    rim_recv,
    pair_send,
    pair_recv,
    out_sem,
):
    group = lax.axis_index("sub")
    block = lax.axis_index("rng")
    partners = [jnp.bitwise_xor(group, 1 << level) for level in range(LEVELS)]

    barrier = pltpu.get_barrier_semaphore()

    def greet(step, carry):
        peer = lax.rem(block + step, sources)
        pl.semaphore_signal(barrier, inc=1, device_id=(group, peer), device_id_type=MESH)
        return carry

    for partner in partners[::-1]:
        pl.semaphore_signal(barrier, inc=1, device_id=(partner, block), device_id_type=MESH)
    lax.fori_loop(1, sources, greet, 0)
    loads = [
        pltpu.make_async_copy(source, target, wide_sem.at[place])
        for place, (source, target) in enumerate(((kernels_far, kernels), (interp_far, interp), (doppler, wide)))
    ]
    for load in loads:
        load.start()
    pl.semaphore_wait(barrier, sources - 1 + LEVELS)

    def turn(step, carry):
        peer = lax.rem(block + step, sources)
        pltpu.make_async_remote_copy(
            src_ref=echoes.at[:, pl.ds(pl.multiple_of(peer * BINS, BINS), BINS)],
            dst_ref=turned.at[block],
            send_sem=turn_sem.at[0],
            recv_sem=turn_sem.at[1],
            device_id=(group, peer),
            device_id_type=MESH,
        ).start()
        return carry

    lax.fori_loop(1, sources, turn, 0)
    stay = pltpu.make_async_copy(
        echoes.at[:, pl.ds(pl.multiple_of(block * BINS, BINS), BINS)], turned.at[block], turn_sem.at[2]
    )
    stay.start()

    loads[0].wait()
    loads[1].wait()
    for level in range(LEVELS):
        offset = offsets[level, 0, group]
        rows = lax.broadcasted_iota(jnp.int32, (TILE, BINS + 2 * BAND_HALF), 0)
        taps = lax.broadcasted_iota(jnp.int32, (TILE, BINS + 2 * BAND_HALF), 1)

        def shift(step, carry, level=level, offset=offset, rows=rows, taps=taps):
            start = pl.multiple_of(step * TILE, TILE)
            pick = jnp.where(rows + start == taps + (TILE - BAND_HALF + offset), 1.0, 0.0).astype(jnp.bfloat16)
            moved = jnp.dot(pick, kernels[level], preferred_element_type=jnp.float32)
            shifted[level, pl.ds(start, TILE), :] = moved.astype(jnp.bfloat16)
            return carry

        lax.fori_loop(0, TILES + 2, shift, 0)

        def choose(step, carry, level=level):
            rows = pl.ds(pl.multiple_of(step * TILE, TILE), TILE)
            zero = interp[level, 0, rows, :].astype(jnp.float32)
            one = interp[level, 1, rows, :].astype(jnp.float32)
            side = jnp.full((TILE, HALF), flags[level, 0, group], jnp.int32)
            chosen[level, 0, rows, :] = jnp.where(side == 1, one, zero).astype(jnp.bfloat16)
            chosen[level, 1, rows, :] = jnp.where(side == 1, zero, one).astype(jnp.bfloat16)
            return carry

        lax.fori_loop(0, ANGLES // TILE, choose, 0)

    rows_at_once = 32

    def tables(step, carry):
        first = pl.multiple_of(step * rows_at_once, rows_at_once)
        angle = lax.broadcasted_iota(jnp.int32, (rows_at_once, BINS), 0) + first
        angle_pos = (angle.astype(jnp.float32) + 0.5) / ANGLES - 0.5
        bins = lax.broadcasted_iota(jnp.int32, (rows_at_once, BINS), 1) + block * BINS
        range_pos = 1.0 + bins.astype(jnp.float32) / total_bins
        for level in range(LEVELS):
            for side, owner in enumerate((group, partners[level])):
                phase = math.pi * shifts[level, owner] * angle_pos * range_pos
                cos_table[level, side, pl.ds(first, rows_at_once), :] = jnp.cos(phase)
                sin_table[level, side, pl.ds(first, rows_at_once), :] = jnp.sin(phase)
        return carry

    lax.fori_loop(0, ANGLES // rows_at_once, tables, 0)

    @pl.when(block == 0)
    def _():
        for level in range(LEVELS):
            left_rim[level] = jnp.zeros((2 * ANGLES, TILE), jnp.bfloat16)

    @pl.when(block == sources - 1)
    def _():
        for level in range(LEVELS):
            right_rim[level] = jnp.zeros((2 * ANGLES, TILE), jnp.bfloat16)

    def to_left(level):
        return pltpu.make_async_remote_copy(
            src_ref=images.at[level, :, pl.ds(0, TILE)],
            dst_ref=right_rim.at[level],
            send_sem=rim_send.at[level, 0],
            recv_sem=rim_recv.at[level, 0],
            device_id=(group, block - 1),
            device_id_type=MESH,
        )

    def to_right(level):
        return pltpu.make_async_remote_copy(
            src_ref=images.at[level, :, pl.ds(BINS - TILE, TILE)],
            dst_ref=left_rim.at[level],
            send_sem=rim_send.at[level, 1],
            recv_sem=rim_recv.at[level, 1],
            device_id=(group, block + 1),
            device_id_type=MESH,
        )

    def send_rims(level, left=True, right=True):
        if left:

            @pl.when(block > 0)
            def _():
                to_left(level).start()

        if right:

            @pl.when(block < sources - 1)
            def _():
                to_right(level).start()

    loads[2].wait()
    stay.wait()
    others = turned.at[pl.ds(0, sources - 1)]
    pltpu.make_async_copy(others, others, turn_sem.at[1]).wait()

    for part in range(2):
        rows = slice(part * ANGLES, part * ANGLES + ANGLES)
        image = jnp.dot(wide[rows, :], turned[...].reshape(2 * PULSES, BINS), preferred_element_type=jnp.float32)
        images[0, rows, :] = image.astype(jnp.bfloat16)
    send_rims(0)

    def to_partner(level, tile):
        return pltpu.make_async_remote_copy(
            src_ref=given.at[level, tile],
            dst_ref=taken.at[level, tile],
            send_sem=pair_send.at[level, tile],
            recv_sem=pair_recv.at[level, tile],
            device_id=(partners[level], block),
            device_id_type=MESH,
        )

    def resample(level, tile):
        if tile == 0:

            @pl.when(block > 0)
            def _():
                to_right(level).wait_recv()

        if tile == TILES - 1:

            @pl.when(block < sources - 1)
            def _():
                to_left(level).wait_recv()

        columns = slice(tile * TILE, tile * TILE + TILE)
        weights = shifted[level, tile * TILE : (tile + 3) * TILE, columns]
        flag = jnp.full((HALF, TILE), flags[level, 0, group], jnp.int32)
        for part in range(2):
            rows = slice(part * ANGLES, part * ANGLES + ANGLES)
            if tile == 0:
                window = jnp.concatenate([left_rim[level, rows, :], images[level, rows, 0 : 2 * TILE]], axis=1)
            elif tile == TILES - 1:
                window = jnp.concatenate([images[level, rows, BINS - 2 * TILE :], right_rim[level, rows, :]], axis=1)
            else:
                window = images[level, rows, (tile - 1) * TILE : (tile + 2) * TILE]
            both = jnp.dot(window, weights, preferred_element_type=jnp.float32)
            values = (both[0:HALF], both[HALF:ANGLES])
            given[level, tile, part] = jnp.where(flag == 1, values[0], values[1]).astype(jnp.bfloat16)
            kept[part, :, columns] = jnp.where(flag == 1, values[1], values[0]).astype(jnp.bfloat16)
        to_partner(level, tile).start()

    def to_out(part, tile):
        return pltpu.make_async_copy(
            total.at[pl.ds(part * ANGLES, ANGLES), pl.ds(tile * TILE, TILE)],
            out.at[part, :, pl.ds(tile * TILE, TILE)],
            out_sem.at[part, tile],
        )

    for tile in ORDERS[0]:
        resample(0, tile)
    for level in range(LEVELS):
        for tile in ORDERS[level]:
            columns = slice(tile * TILE, tile * TILE + TILE)
            matrix = chosen[level, 0]
            real = jnp.dot(matrix, kept[0, :, columns], preferred_element_type=jnp.float32)
            imag = jnp.dot(matrix, kept[1, :, columns], preferred_element_type=jnp.float32)
            cosine = cos_table[level, 0, :, columns]
            sine = sin_table[level, 0, :, columns]
            total[0:ANGLES, columns] = real * cosine - imag * sine
            total[ANGLES : 2 * ANGLES, columns] = real * sine + imag * cosine

        for order, tile in enumerate(ORDERS[level]):
            columns = slice(tile * TILE, tile * TILE + TILE)
            to_partner(level, tile).wait_recv()

            matrix = chosen[level, 1]
            real = jnp.dot(matrix, taken[level, tile, 0], preferred_element_type=jnp.float32)
            imag = jnp.dot(matrix, taken[level, tile, 1], preferred_element_type=jnp.float32)
            cosine = cos_table[level, 1, :, columns]
            sine = sin_table[level, 1, :, columns]
            high = total[0:ANGLES, columns] + (real * cosine - imag * sine)
            low = total[ANGLES : 2 * ANGLES, columns] + (real * sine + imag * cosine)
            if level + 1 < LEVELS:
                images[level + 1, 0:ANGLES, columns] = high.astype(jnp.bfloat16)
                images[level + 1, ANGLES : 2 * ANGLES, columns] = low.astype(jnp.bfloat16)
            else:
                total[0:ANGLES, columns] = high
                total[ANGLES : 2 * ANGLES, columns] = low

            if level + 1 < LEVELS:
                send_rims(level + 1, left=tile == 0, right=tile == TILES - 1)
                if order == 2:
                    resample(level + 1, ORDERS[level + 1][0])
                if order == 3:
                    for later in ORDERS[level + 1][1:]:
                        resample(level + 1, later)
            else:
                for part in range(2):
                    to_out(part, tile).start()

    for level in range(LEVELS):
        for tile in range(TILES):
            to_partner(level, tile).wait_send()

        @pl.when(block > 0)
        def _(level=level):
            to_left(level).wait_send()

        @pl.when(block < sources - 1)
        def _(level=level):
            to_right(level).wait_send()

    pltpu.make_async_copy(others, others, turn_sem.at[0]).wait()
    for tile in range(TILES):
        for part in range(2):
            to_out(part, tile).wait()


def on_device(doppler, sources, echoes, fore_flag, band_offset, angle_interp, range_kernel, center_shift):
    pulses = echoes.shape[1]
    total_bins = echoes.shape[2]
    any_space = pl.BlockSpec(memory_space=pl.ANY)
    smem = pl.BlockSpec(memory_space=pltpu.SMEM)
    bf16 = jnp.bfloat16
    return pl.pallas_call(
        functools.partial(kernel, sources, total_bins),
        out_shape=jax.ShapeDtypeStruct((2, ANGLES, BINS), jnp.float32),
        in_specs=[any_space, any_space, any_space, any_space, smem, smem, smem],
        out_specs=any_space,
        scratch_shapes=[
            pltpu.VMEM((sources, 2 * pulses, BINS), bf16),
            pltpu.VMEM((2 * ANGLES, 2 * PULSES), bf16),
            pltpu.VMEM(range_kernel.shape, bf16),
            pltpu.VMEM(angle_interp.shape, bf16),
            pltpu.VMEM((LEVELS, BINS + 2 * TILE, BINS), bf16),
            pltpu.VMEM((LEVELS, 2, ANGLES, HALF), bf16),
            pltpu.VMEM((LEVELS, 2 * ANGLES, BINS), bf16),
            pltpu.VMEM((LEVELS, 2 * ANGLES, TILE), bf16),
            pltpu.VMEM((LEVELS, 2 * ANGLES, TILE), bf16),
            pltpu.VMEM((LEVELS, TILES, 2, HALF, TILE), bf16),
            pltpu.VMEM((2, HALF, BINS), bf16),
            pltpu.VMEM((LEVELS, TILES, 2, HALF, TILE), bf16),
            pltpu.VMEM((2 * ANGLES, BINS), jnp.float32),
            pltpu.VMEM((LEVELS, 2, ANGLES, BINS), jnp.float32),
            pltpu.VMEM((LEVELS, 2, ANGLES, BINS), jnp.float32),
            pltpu.SemaphoreType.DMA((3,)),
            pltpu.SemaphoreType.DMA((3,)),
            pltpu.SemaphoreType.DMA((LEVELS, 2)),
            pltpu.SemaphoreType.DMA((LEVELS, 2)),
            pltpu.SemaphoreType.DMA((LEVELS, TILES)),
            pltpu.SemaphoreType.DMA((LEVELS, TILES)),
            pltpu.SemaphoreType.DMA((2, TILES)),
        ],
        compiler_params=pltpu.CompilerParams(collective_id=0, has_side_effects=True, vmem_limit_bytes=60 * 2**20),
    )(
        echoes.reshape(2 * pulses, total_bins),
        jnp.asarray(doppler),
        range_kernel,
        angle_interp,
        fore_flag.transpose(0, 2, 1),
        band_offset.transpose(0, 2, 1),
        center_shift,
    )


def solution(mesh):
    sources = mesh.shape["rng"]
    placed = (
        P(None, ("sub", "rng"), None),
        P(None, None, "rng"),
        P(None, None, "rng"),
        P(),
        P(),
        P(),
    )
    body = functools.partial(on_device, doppler_constant(sources), sources)
    return jax.shard_map(body, mesh=mesh, in_specs=placed, out_specs=P(None, "sub", "rng"), check_vma=False)
```
